128 devices in a mesh: mem: 4 (over y), col: 32 (over z, x, core).
Axes of the slice: x: 4, y: 4, z: 4, core: 2. Of those that a mesh axis runs over, the one named last changes fastest.
Arguments:
- ensemble: bfloat16 [256, 3, 128, 4096], P('mem', None, None, 'col'), may hold values from -6 to 6
- increment: bfloat16 [3, 128, 4096], P(None, 'mem', 'col'), may hold values from -6 to 6
- vert_root: bfloat16 [3, 128, 128], replicated, may hold values from -1 to 2, as said below
- tiles: bfloat16 [32, 8, 128, 128], replicated, may hold values from -2 to 3, as said below
- tile_col: int32 [32, 8], replicated, may hold values from 0 to 31, as said below
- level_reach: int32 [128], replicated, may hold values from 2 to 8, as said below
Outputs:
- covaried: bfloat16 [3, 128, 4096], P(None, 'mem', 'col')
The draws below stay inside these ranges and needn't reach their ends.
Inputs may be any that keep to these rules, and one draw needn't show every extreme that they name: `vert_root`: each variable's matrix is the identity plus bounded noise. `tiles`: slot 0 of block row r is the identity plus bounded noise; the other slots are bounded noise. `tile_col`: each row r names K distinct column blocks; slot 0 names r itself. `level_reach`: level 0 uses 2 slots and the top level uses all 8; the count mostly rises with the level.
All inputs are finite; a program needn't handle non-finite values.
Results may differ from the reference program's by a relative error of at most 0.012.
Values may be sent and summed in bfloat16 or wider, within the bound.
No kernel may reach another device: no remote copies, remote signals or barrier semaphores. Data moves between devices by JAX's collectives and lax.ppermute only.
A program may use at most 128 MiB of HBM per device.

```python
import jax
import jax.numpy as jnp
from jax import lax

NV = 3
NL = 128
TILE = 128
K = 8
MEMBERS = 256
BLOCKS = 32
NC = 4096


def draw_vert_root(key, part):
    noise = jnp.clip(jax.random.normal(key, (NV, NL, NL), jnp.float32), -6.0, 6.0)
    eye = jnp.eye(NL, dtype=jnp.float32)
    return (eye[None] + 0.5 * noise / jnp.sqrt(NL * 1.0)).astype(jnp.bfloat16)


def draw_tiles(key, part):
    noise = jnp.clip(jax.random.normal(key, (BLOCKS, K, TILE, TILE), jnp.float32), -6.0, 6.0)
    scaled = noise / jnp.sqrt(TILE * K * 1.0)
    first = (jnp.arange(K) == 0).astype(jnp.float32)
    eye = jnp.eye(TILE, dtype=jnp.float32)
    return (scaled + first[None, :, None, None] * eye[None, None]).astype(jnp.bfloat16)


def draw_tile_col(key, part):

    def one_row(index):
        shuffled = jax.random.permutation(jax.random.fold_in(key, index), BLOCKS - 1) + 1
        offsets = jnp.concatenate([jnp.zeros((1,), jnp.int32), shuffled[:K - 1].astype(jnp.int32)])
        return (index + offsets) % BLOCKS
    return jax.vmap(one_row)(jnp.arange(BLOCKS, dtype=jnp.int32)).astype(jnp.int32)


def draw_level_reach(key, part):
    levels = jnp.arange(NL, dtype=jnp.int32)
    base = 2 + (K - 2) * levels // (NL - 1)
    jitter = jax.random.randint(key, (NL,), -1, 1).astype(jnp.int32)
    reach = jnp.clip(base + jitter, 2, K)
    return jnp.where(levels == NL - 1, K, reach).astype(jnp.int32)


def shard_levels(own_key, extent, pieces, low, high):
    factor_of, own = 1.0, jax.random.fold_in(own_key, 6)
    for position, parts in pieces:
        heights = jnp.exp(jax.random.uniform(jax.random.fold_in(own, position), (parts,), jnp.float32, low / len(pieces), high / len(pieces)))
        factor_of = factor_of * jnp.repeat(heights, extent[position] // parts).reshape([-1 if axis == position else 1 for axis in range(len(extent))])
    return factor_of


def centred(stream_key, extent, spread, limit, pieces=(), kind=jnp.bfloat16):
    entries = spread * jax.random.normal(stream_key, extent, jnp.float32)
    if pieces:
        entries = entries * shard_levels(stream_key, extent, pieces, -0.22, 0.18)
    return jnp.clip(entries, -limit, limit).astype(kind)


def setup_inputs(seed: int = 0) -> dict:
    splits = jax.random.split(jax.random.key(seed), 7)
    return {
        "ensemble": centred(splits[0], (MEMBERS, NV, NL, NC), 1.0, 6.0, ((0, 4), (3, 32))),
        "increment": centred(splits[1], (NV, NL, NC), 1.0, 6.0, ((1, 4), (2, 32))),
        "vert_root": draw_vert_root(jax.random.fold_in(splits[6], 71), 0),
        "tiles": draw_tiles(jax.random.fold_in(splits[6], 71), 0),
        "tile_col": draw_tile_col(jax.random.fold_in(splits[6], 71), 0),
        "level_reach": draw_level_reach(jax.random.fold_in(splits[6], 71), 0),
    }


def reference(ensemble, increment, vert_root, tiles, tile_col, level_reach):
    vertical_factor = vert_root.astype(jnp.float32)
    slots = jnp.arange(K, dtype=jnp.int32)
    active = (slots[None, :] < level_reach[:, None]).astype(jnp.float32)
    tile_f = tiles.astype(jnp.float32)
    incr_f = increment.astype(jnp.float32)

    def member_step(total, member):
        member_f = member.astype(jnp.float32)
        weighted_increment = (member_f * incr_f).astype(jnp.bfloat16)
        lifted_increment = jnp.einsum('qzw,qzn->qwn', vertical_factor, weighted_increment.astype(jnp.float32)).astype(jnp.bfloat16)
        grid = lifted_increment.astype(jnp.float32).reshape(NV, NL, BLOCKS, TILE)
        spread_increment = jnp.zeros((NV, NL, BLOCKS, TILE), jnp.float32)
        for slot in range(K):
            picked = jnp.take(grid, tile_col[:, slot], axis=2)
            term = jnp.einsum('vlbi,bij->vlbj', picked, tile_f[:, slot])
            spread_increment = spread_increment + term * active[:, slot][None, :, None, None]
        spread_increment = spread_increment.reshape(NV, NL, NC).astype(jnp.bfloat16)
        lowered_increment = jnp.einsum('duw,dws->dus', vertical_factor, spread_increment.astype(jnp.float32))
        return total + member_f * lowered_increment, None

    total, _ = lax.scan(member_step, jnp.zeros((NV, NL, NC), jnp.float32), ensemble)
    return (total / (MEMBERS - 1)).astype(jnp.bfloat16)
```

```python
import functools

import jax
import jax.numpy as jnp
from jax import lax
from jax.experimental import pallas as pl
from jax.experimental.pallas import tpu as pltpu
from jax.sharding import PartitionSpec as P

BF = jnp.bfloat16
F32 = jnp.float32
CORES = 2


def member_kernel(
    where_ref, cols_ref, ens_ref, mine_ref, other_ref, vt_ref, vn_ref, mask_ref, tiles_ref,
    near_ref, far_ref, tile_buf, lifted, sems, *, var, slot_of_var,
):
    members = ens_ref.shape[1]
    n_blocks = ens_ref.shape[0]
    levels = ens_ref.shape[3]
    width = ens_ref.shape[4]
    y_n, z_n, x_n = mine_ref.shape[0], mine_ref.shape[1], mine_ref.shape[2]
    part_l = mine_ref.shape[4]
    slots = cols_ref.shape[1]
    pairs = slots // 2
    my_y, my_z, my_x, my_c = where_ref[0], where_ref[1], where_ref[2], where_ref[3]
    n_copies = sems.shape[0]
    per_copy = n_blocks // n_copies

    def tile_copy(piece):
        span = pl.ds(piece * per_copy, per_copy)
        return pltpu.make_async_copy(tiles_ref.at[span], tile_buf.at[span], sems.at[piece])

    for piece in range(n_copies):
        tile_copy(piece).start()

    def seat_of(step):
        off_z, off_x = step // x_n, step % x_n
        z = lax.rem(my_z + off_z, z_n)
        x = lax.rem(my_x + off_x, x_n)
        return off_z, off_x, (z * x_n + x) * CORES

    def lift_block(source_ref, block, in_z, in_x):
        halves = []
        for m in range(members):
            bands = []
            for quarter in range(y_n):
                off_y = lax.rem(my_y - quarter + y_n, y_n)
                incr = source_ref[off_y, in_z, in_x, var].astype(F32)
                rows = ens_ref[block, m, slot_of_var, quarter * part_l:(quarter + 1) * part_l, :]
                bands.append((rows.astype(F32) * incr).astype(BF))
            halves.append(jnp.concatenate(bands, axis=0))
        weighted = jnp.concatenate(halves, axis=1)
        lift = jnp.dot(vt_ref[var], weighted, preferred_element_type=F32).astype(BF)
        for m in range(members):
            lifted[block, m * levels:(m + 1) * levels, :] = lift[:, m * width:(m + 1) * width]

    def lift_step(step, carry):
        off_z, off_x, base = seat_of(step)
        in_z = lax.rem(z_n - off_z, z_n)
        in_x = lax.rem(x_n - off_x, x_n)
        lift_block(mine_ref, base + my_c, in_z, in_x)
        lift_block(other_ref, base + 1 - my_c, in_z, in_x)
        return carry

    lax.fori_loop(0, n_blocks // CORES, lift_step, 0)
    for piece in range(n_copies):
        tile_copy(piece).wait()

    def spread_block(target_ref, block, off_z, off_x):
        acc = None
        for pair in range(pairs):
            first = lifted[cols_ref[block, 2 * pair]]
            second = lifted[cols_ref[block, 2 * pair + 1]]
            both = jnp.concatenate([first, second], axis=1)
            if pair > 0:
                both = both * mask_ref[pair - 1]
            term = jnp.dot(
                both, tile_buf[block, 2 * pair * width:2 * (pair + 1) * width, :],
                preferred_element_type=F32,
            )
            acc = term if acc is None else acc + term
        spread = acc.astype(BF)
        beside = jnp.concatenate(
            [spread[m * levels:(m + 1) * levels, :] for m in range(members)], axis=1
        )
        lowered = jnp.dot(vn_ref[var], beside, preferred_element_type=F32)
        total = None
        for m in range(members):
            term = ens_ref[block, m, slot_of_var].astype(F32) * lowered[:, m * width:(m + 1) * width]
            total = term if total is None else total + term
        total = total.astype(BF)
        for quarter in range(y_n):
            off_y = lax.rem(quarter - my_y + y_n, y_n)
            target_ref[off_y, off_z, off_x] = total[quarter * part_l:(quarter + 1) * part_l, :]

    def spread_step(step, carry):
        off_z, off_x, base = seat_of(step)
        spread_block(near_ref, base + my_c, off_z, off_x)
        spread_block(far_ref, base + 1 - my_c, off_z, off_x)
        return carry

    lax.fori_loop(0, n_blocks // CORES, spread_step, 0)


def on_device(
    ensemble, increment, vert_root, tiles, tile_col, level_reach, *, y_n, z_n, x_n
):
    columns = lax.axis_size("col")
    members_all = ensemble.shape[0] * lax.axis_size("mem")
    members = ensemble.shape[0] // columns
    n_var, levels, width = ensemble.shape[1:]
    part_l = increment.shape[1]
    slots = tiles.shape[1]
    col = lax.axis_index("col")
    my_y = lax.axis_index("mem")
    my_z, my_x, my_c = col // (x_n * CORES), (col // CORES) % x_n, col % CORES
    where = jnp.stack([my_y, my_z, my_x, my_c]).astype(jnp.int32)

    def seat(z, x, c):
        return ((z % z_n) * x_n + x % x_n) * CORES + c

    seats = [(z, x, c) for z in range(z_n) for x in range(x_n) for c in range(CORES)]

    def shift_y(a, s):
        return lax.ppermute(a, "mem", [(i, (i + s) % y_n) for i in range(y_n)])

    def shift_z(a, s):
        return lax.ppermute(a, "col", [(seat(*p), seat(p[0] + s, p[1], p[2])) for p in seats])

    def shift_x(a, s):
        return lax.ppermute(a, "col", [(seat(*p), seat(p[0], p[1] + s, p[2])) for p in seats])

    def swap(a):
        return lax.ppermute(a, "col", [(seat(*p), seat(p[0], p[1], 1 - p[2])) for p in seats])

    def collect(a, shift, n):
        return jnp.stack([a] + [shift(a, s) for s in range(1, n)])

    by_member = ensemble.reshape(columns, members, n_var, levels, width)
    groups = ((0, 1), (2,))
    arrived, where_var = [], {}
    for index, group in enumerate(groups):
        piece = by_member[:, :, group[0]:group[-1] + 1]
        if arrived:
            piece, arrived[-1] = lax.optimization_barrier((piece, arrived[-1]))
        arrived.append(lax.all_to_all(piece, "col", 0, 0))
        for place, var in enumerate(group):
            where_var[var] = (index, place)

    mine = collect(increment, shift_x, x_n)
    mine = collect(mine, shift_z, z_n)
    mine = collect(mine, shift_y, y_n)
    other = swap(mine)

    vert_t = jnp.swapaxes(vert_root, 1, 2)
    active = (
        jnp.arange(2, slots, dtype=jnp.int32)[:, None] < level_reach[None, :]
    ).astype(BF).reshape(slots // 2 - 1, 2, levels)
    active = jnp.swapaxes(active, 1, 2)
    mask = jnp.broadcast_to(
        active[:, None, :, :, None], (slots // 2 - 1, members, levels, 2, width)
    ).reshape(slots // 2 - 1, members * levels, 2 * width)
    flat_tiles = tiles.reshape(columns, slots * width, width)

    vmem = pl.BlockSpec(memory_space=pltpu.VMEM)
    smem = pl.BlockSpec(memory_space=pltpu.SMEM)
    out = jax.ShapeDtypeStruct((y_n, z_n, x_n, part_l, width), BF)

    def add(parts):
        total = parts[0].astype(F32)
        for p in parts[1:]:
            total = total + p.astype(F32)
        return total

    held = []
    for var in range(n_var):
        index, place = where_var[var]
        near, far = pl.pallas_call(
            functools.partial(member_kernel, var=var, slot_of_var=place),
            out_shape=(out, out),
            in_specs=[smem, smem, vmem, vmem, vmem, vmem, vmem, vmem,
                      pl.BlockSpec(memory_space=pl.ANY)],
            out_specs=(vmem, vmem),
            scratch_shapes=[
                pltpu.VMEM(flat_tiles.shape, BF),
                pltpu.VMEM((columns, members * levels, width), BF),
                pltpu.SemaphoreType.DMA((4,)),
            ],
            compiler_params=pltpu.CompilerParams(vmem_limit_bytes=40 << 20),
            name=f"members_{var}",
        )(where, tile_col, arrived[index], mine, other, vert_t, vert_root, mask, flat_tiles)
        chip = add([near, swap(far)]).astype(BF)
        held.append(add([chip[0]] + [shift_y(chip[s], s) for s in range(1, y_n)]).astype(BF))
    held = jnp.stack(held, axis=2)
    held = add([held[0]] + [shift_z(held[s], s) for s in range(1, z_n)]).astype(BF)
    held = add([held[0]] + [shift_x(held[s], s) for s in range(1, x_n)])
    return (held / (members_all - 1)).astype(BF)


def solution(mesh):
    y_n = mesh.shape["mem"]
    side = int(round((mesh.shape["col"] // CORES) ** 0.5))
    placed = (P("mem", None, None, "col"), P(None, "mem", "col"), P(), P(), P(), P())
    return jax.shard_map(
        functools.partial(on_device, y_n=y_n, z_n=side, x_n=side),
        mesh=mesh, in_specs=placed, out_specs=P(None, "mem", "col"), check_vma=False,
    )
```

```python
import functools

import jax
import jax.numpy as jnp
from jax import lax
from jax.experimental import pallas as pl
from jax.experimental.pallas import tpu as pltpu
from jax.sharding import PartitionSpec as P

BF = jnp.bfloat16
F32 = jnp.float32
CORES = 2
FLOOR = 2


def member_kernel(
    where_ref, cols_ref, ens_ref, mine_ref, other_ref, vt_ref, vn_ref, mask_ref, tiles_ref,
    near_ref, far_ref, tile_buf, lifted, sems, *, var, slot_of_var,
):
    members = ens_ref.shape[1]
    n_blocks = ens_ref.shape[0]
    levels = ens_ref.shape[3]
    width = ens_ref.shape[4]
    y_n, z_n, x_n = mine_ref.shape[0], mine_ref.shape[1], mine_ref.shape[2]
    part_l = mine_ref.shape[4]
    slots = cols_ref.shape[1]
    my_y, my_z, my_x, my_c = where_ref[0], where_ref[1], where_ref[2], where_ref[3]
    n_copies = sems.shape[0]
    per_copy = n_blocks // n_copies

    def tile_copy(piece):
        span = pl.ds(piece * per_copy, per_copy)
        return pltpu.make_async_copy(tiles_ref.at[span], tile_buf.at[span], sems.at[piece])

    for piece in range(n_copies):
        tile_copy(piece).start()

    def seat_of(step):
        off_z, off_x = step // x_n, step % x_n
        z = lax.rem(my_z + off_z, z_n)
        x = lax.rem(my_x + off_x, x_n)
        return off_z, off_x, (z * x_n + x) * CORES

    def lift_block(source_ref, block, in_z, in_x):
        halves = []
        for m in range(members):
            bands = []
            for quarter in range(y_n):
                off_y = lax.rem(my_y - quarter + y_n, y_n)
                incr = source_ref[off_y, in_z, in_x, var].astype(F32)
                rows = ens_ref[block, m, slot_of_var, quarter * part_l:(quarter + 1) * part_l, :]
                bands.append((rows.astype(F32) * incr).astype(BF))
            halves.append(jnp.concatenate(bands, axis=0))
        weighted = jnp.concatenate(halves, axis=1)
        lift = jnp.dot(vt_ref[var], weighted, preferred_element_type=F32).astype(BF)
        for m in range(members):
            lifted[block, :, m * levels:(m + 1) * levels] = jnp.swapaxes(
                lift[:, m * width:(m + 1) * width], 0, 1
            )

    def lift_step(step, carry):
        off_z, off_x, base = seat_of(step)
        in_z = lax.rem(z_n - off_z, z_n)
        in_x = lax.rem(x_n - off_x, x_n)
        lift_block(mine_ref, base + my_c, in_z, in_x)
        lift_block(other_ref, base + 1 - my_c, in_z, in_x)
        return carry

    lax.fori_loop(0, n_blocks // CORES, lift_step, 0, unroll=2)
    for piece in range(n_copies):
        tile_copy(piece).wait()

    def spread_block(target_ref, block, off_z, off_x):
        parts = []
        for slot in range(slots):
            picked = lifted[cols_ref[block, slot]]
            if slot >= FLOOR:
                picked = picked * mask_ref[slot - FLOOR]
            parts.append(picked)
        spread = jnp.dot(
            tile_buf[block], jnp.concatenate(parts, axis=0), preferred_element_type=F32
        ).astype(BF)
        beside = jnp.concatenate(
            [spread[:, m * levels:(m + 1) * levels] for m in range(members)], axis=0
        )
        lowered = lax.dot_general(
            vn_ref[var], beside, (((1,), (1,)), ((), ())), preferred_element_type=F32
        )
        total = None
        for m in range(members):
            term = ens_ref[block, m, slot_of_var].astype(F32) * lowered[:, m * width:(m + 1) * width]
            total = term if total is None else total + term
        total = total.astype(BF)
        for quarter in range(y_n):
            off_y = lax.rem(quarter - my_y + y_n, y_n)
            target_ref[off_y, off_z, off_x] = total[quarter * part_l:(quarter + 1) * part_l, :]

    def spread_step(step, carry):
        off_z, off_x, base = seat_of(step)
        spread_block(near_ref, base + my_c, off_z, off_x)
        spread_block(far_ref, base + 1 - my_c, off_z, off_x)
        return carry

    lax.fori_loop(0, n_blocks // CORES, spread_step, 0, unroll=2)


def on_device(
    ensemble, increment, vert_root, tiles, tile_col, level_reach, *, y_n, z_n, x_n
):
    columns = lax.axis_size("col")
    members_all = ensemble.shape[0] * lax.axis_size("mem")
    members = ensemble.shape[0] // columns
    n_var, levels, width = ensemble.shape[1:]
    part_l = increment.shape[1]
    slots = tiles.shape[1]
    col = lax.axis_index("col")
    my_y = lax.axis_index("mem")
    my_z, my_x, my_c = col // (x_n * CORES), (col // CORES) % x_n, col % CORES
    where = jnp.stack([my_y, my_z, my_x, my_c]).astype(jnp.int32)

    def seat(z, x, c):
        return ((z % z_n) * x_n + x % x_n) * CORES + c

    seats = [(z, x, c) for z in range(z_n) for x in range(x_n) for c in range(CORES)]

    def shift_y(a, s):
        return lax.ppermute(a, "mem", [(i, (i + s) % y_n) for i in range(y_n)])

    def shift_z(a, s):
        return lax.ppermute(a, "col", [(seat(*p), seat(p[0] + s, p[1], p[2])) for p in seats])

    def shift_x(a, s):
        return lax.ppermute(a, "col", [(seat(*p), seat(p[0], p[1] + s, p[2])) for p in seats])

    def swap(a):
        return lax.ppermute(a, "col", [(seat(*p), seat(p[0], p[1], 1 - p[2])) for p in seats])

    def collect(a, shift, n):
        return jnp.stack([a] + [shift(a, s) for s in range(1, n)])

    by_member = ensemble.reshape(columns, members, n_var, levels, width)
    groups = ((0, 1), (2,))
    pieces = [by_member[:, :, group[0]:group[-1] + 1] for group in groups]
    where_var = {
        var: (index, place) for index, group in enumerate(groups) for place, var in enumerate(group)
    }

    mine = collect(increment, shift_x, x_n)
    mine = collect(mine, shift_z, z_n)
    pieces[0], mine = lax.optimization_barrier((pieces[0], mine))
    arrived = [lax.all_to_all(pieces[0], "col", 0, 0)]
    mine, pieces[1], tiles = lax.optimization_barrier((mine, pieces[1], tiles))
    turned_tiles = jnp.transpose(tiles, (0, 3, 1, 2)).reshape(columns, width, slots * width)
    mine = collect(mine, shift_y, y_n)
    mine, turned_tiles = lax.optimization_barrier((mine, turned_tiles))
    other = swap(mine)
    pieces[1], arrived[0] = lax.optimization_barrier((pieces[1], arrived[0]))
    arrived.append(lax.all_to_all(pieces[1], "col", 0, 0))

    vert_t = jnp.swapaxes(vert_root, 1, 2)
    active = (
        jnp.arange(FLOOR, slots, dtype=jnp.int32)[:, None] < level_reach[None, :]
    ).astype(BF)
    mask = jnp.tile(active, (1, members))[:, None, :]

    vmem = pl.BlockSpec(memory_space=pltpu.VMEM)
    smem = pl.BlockSpec(memory_space=pltpu.SMEM)
    out = jax.ShapeDtypeStruct((y_n, z_n, x_n, part_l, width), BF)

    def add(parts):
        total = parts[0].astype(F32)
        for p in parts[1:]:
            total = total + p.astype(F32)
        return total

    held = []
    for var in range(n_var):
        index, place = where_var[var]
        if index and place == 0:
            arrived[index], *held = lax.optimization_barrier((arrived[index], *held))
        near, far = pl.pallas_call(
            functools.partial(member_kernel, var=var, slot_of_var=place),
            out_shape=(out, out),
            in_specs=[smem, smem, vmem, vmem, vmem, vmem, vmem, vmem,
                      pl.BlockSpec(memory_space=pl.ANY)],
            out_specs=(vmem, vmem),
            scratch_shapes=[
                pltpu.VMEM(turned_tiles.shape, BF),
                pltpu.VMEM((columns, width, members * levels), BF),
                pltpu.SemaphoreType.DMA((4,)),
            ],
            compiler_params=pltpu.CompilerParams(vmem_limit_bytes=40 << 20),
            name=f"members_{var}",
        )(where, tile_col, arrived[index], mine, other, vert_t, vert_root, mask, turned_tiles)
        chip = add([near, swap(far)]).astype(BF)
        held.append(add([chip[0]] + [shift_y(chip[s], s) for s in range(1, y_n)]).astype(BF))
    held = jnp.stack(held, axis=2)
    held = add([held[0]] + [shift_z(held[s], s) for s in range(1, z_n)]).astype(BF)
    held = add([held[0]] + [shift_x(held[s], s) for s in range(1, x_n)])
    return (held / (members_all - 1)).astype(BF)


def solution(mesh):
    y_n = mesh.shape["mem"]
    side = int(round((mesh.shape["col"] // CORES) ** 0.5))
    placed = (P("mem", None, None, "col"), P(None, "mem", "col"), P(), P(), P(), P())
    return jax.shard_map(
        functools.partial(on_device, y_n=y_n, z_n=side, x_n=side),
        mesh=mesh, in_specs=placed, out_specs=P(None, "mem", "col"), check_vma=False,
    )
```

```python
import functools

import jax
import jax.numpy as jnp
from jax import lax
from jax.experimental import pallas as pl
from jax.experimental.pallas import tpu as pltpu
from jax.sharding import PartitionSpec as P


BF = jnp.bfloat16
F32 = jnp.float32
CORES = 2
FLOOR = 2
UNROLL = 4


def member_kernel(
    where_ref, cols_ref, ens_ref, mine_ref, other_ref, vt_ref, vn_ref, mask_ref, tiles_ref,
    near_ref, far_ref, tile_buf, lifted, spread_buf, sems, *, var, slot_of_var,
):
    members = ens_ref.shape[1]
    n_blocks = ens_ref.shape[0]
    levels = ens_ref.shape[3]
    width = ens_ref.shape[4]
    y_n, z_n, x_n = mine_ref.shape[0], mine_ref.shape[1], mine_ref.shape[2]
    part_l = mine_ref.shape[4]
    slots = cols_ref.shape[1]
    my_y, my_z, my_x, my_c = where_ref[0], where_ref[1], where_ref[2], where_ref[3]
    n_copies = sems.shape[0]
    per_copy = n_blocks // n_copies

    def tile_copy(piece):
        span = pl.ds(piece * per_copy, per_copy)
        return pltpu.make_async_copy(tiles_ref.at[span], tile_buf.at[span], sems.at[piece])

    for piece in range(n_copies):
        tile_copy(piece).start()

    def seat_of(step):
        off_z, off_x = step // x_n, step % x_n
        z = lax.rem(my_z + off_z, z_n)
        x = lax.rem(my_x + off_x, x_n)
        return off_z, off_x, (z * x_n + x) * CORES

    def lift_block(source_ref, block, in_z, in_x):
        halves = []
        for m in range(members):
            bands = []
            for quarter in range(y_n):
                off_y = lax.rem(my_y - quarter + y_n, y_n)
                incr = source_ref[off_y, in_z, in_x, var].astype(F32)
                rows = ens_ref[block, m, slot_of_var, quarter * part_l:(quarter + 1) * part_l, :]
                bands.append((rows.astype(F32) * incr).astype(BF))
            halves.append(jnp.concatenate(bands, axis=0))
        weighted = jnp.concatenate(halves, axis=1)
        lift = jnp.dot(vt_ref[var], weighted, preferred_element_type=F32).astype(BF)
        for m in range(members):
            lifted[block, :, m * levels:(m + 1) * levels] = jnp.swapaxes(
                lift[:, m * width:(m + 1) * width], 0, 1
            )

    def lift_step(step, carry):
        off_z, off_x, base = seat_of(step)
        in_z = lax.rem(z_n - off_z, z_n)
        in_x = lax.rem(x_n - off_x, x_n)
        lift_block(mine_ref, base + my_c, in_z, in_x)
        lift_block(other_ref, base + 1 - my_c, in_z, in_x)
        return carry

    lax.fori_loop(0, n_blocks // CORES, lift_step, 0, unroll=2)
    for piece in range(n_copies):
        tile_copy(piece).wait()

    def spread_block(block):
        parts = []
        for slot in range(slots):
            picked = lifted[cols_ref[block, slot]]
            if slot >= FLOOR:
                picked = picked * mask_ref[slot - FLOOR]
            parts.append(picked)
        spread = jnp.dot(
            tile_buf[block], jnp.concatenate(parts, axis=0), preferred_element_type=F32
        ).astype(BF)
        for m in range(members):
            spread_buf[block, m * width:(m + 1) * width, :] = spread[:, m * levels:(m + 1) * levels]

    def spread_step(step, carry):
        spread_block(step)
        return carry

    lax.fori_loop(0, n_blocks, spread_step, 0, unroll=UNROLL)

    def lower_block(target_ref, block, off_z, off_x):
        beside = spread_buf[block]
        lowered = lax.dot_general(
            vn_ref[var], beside, (((1,), (1,)), ((), ())), preferred_element_type=F32
        )
        total = None
        for m in range(members):
            term = ens_ref[block, m, slot_of_var].astype(F32) * lowered[:, m * width:(m + 1) * width]
            total = term if total is None else total + term
        total = total.astype(BF)
        for quarter in range(y_n):
            off_y = lax.rem(quarter - my_y + y_n, y_n)
            target_ref[off_y, off_z, off_x] = total[quarter * part_l:(quarter + 1) * part_l, :]

    def lower_step(step, carry):
        off_z, off_x, base = seat_of(step)
        lower_block(near_ref, base + my_c, off_z, off_x)
        lower_block(far_ref, base + 1 - my_c, off_z, off_x)
        return carry

    lax.fori_loop(0, n_blocks // CORES, lower_step, 0, unroll=2)


def on_device(
    ensemble, increment, vert_root, tiles, tile_col, level_reach, *, y_n, z_n, x_n
):
    columns = lax.axis_size("col")
    members_all = ensemble.shape[0] * lax.axis_size("mem")
    members = ensemble.shape[0] // columns
    n_var, levels, width = ensemble.shape[1:]
    part_l = increment.shape[1]
    slots = tiles.shape[1]
    col = lax.axis_index("col")
    my_y = lax.axis_index("mem")
    my_z, my_x, my_c = col // (x_n * CORES), (col // CORES) % x_n, col % CORES
    where = jnp.stack([my_y, my_z, my_x, my_c]).astype(jnp.int32)

    def seat(z, x, c):
        return ((z % z_n) * x_n + x % x_n) * CORES + c

    seats = [(z, x, c) for z in range(z_n) for x in range(x_n) for c in range(CORES)]

    def shift_y(a, s):
        return lax.ppermute(a, "mem", [(i, (i + s) % y_n) for i in range(y_n)])

    def shift_z(a, s):
        return lax.ppermute(a, "col", [(seat(*p), seat(p[0] + s, p[1], p[2])) for p in seats])

    def shift_x(a, s):
        return lax.ppermute(a, "col", [(seat(*p), seat(p[0], p[1] + s, p[2])) for p in seats])

    def swap(a):
        return lax.ppermute(a, "col", [(seat(*p), seat(p[0], p[1], 1 - p[2])) for p in seats])

    def collect(a, shift, n):
        return jnp.stack([a] + [shift(a, s) for s in range(1, n)])

    by_member = ensemble.reshape(columns, members, n_var, levels, width)
    groups = ((0, 1), (2,))
    pieces = [by_member[:, :, group[0]:group[-1] + 1] for group in groups]
    where_var = {
        var: (index, place) for index, group in enumerate(groups) for place, var in enumerate(group)
    }

    mine = collect(increment, shift_x, x_n)
    pieces[0], mine = lax.optimization_barrier((pieces[0], mine))
    mine = collect(mine, shift_z, z_n)
    arrived = [lax.all_to_all(pieces[0], "col", 0, 0)]
    mine, pieces[1], tiles = lax.optimization_barrier((mine, pieces[1], tiles))
    turned_tiles = jnp.transpose(tiles, (0, 3, 1, 2)).reshape(columns, width, slots * width)
    mine = collect(mine, shift_y, y_n)
    mine, turned_tiles = lax.optimization_barrier((mine, turned_tiles))
    other = swap(mine)
    pieces[1], arrived[0] = lax.optimization_barrier((pieces[1], arrived[0]))
    arrived.append(lax.all_to_all(pieces[1], "col", 0, 0))

    vert_t = jnp.swapaxes(vert_root, 1, 2)
    active = (
        jnp.arange(FLOOR, slots, dtype=jnp.int32)[:, None] < level_reach[None, :]
    ).astype(BF)
    mask = jnp.tile(active, (1, members))[:, None, :]

    vmem = pl.BlockSpec(memory_space=pltpu.VMEM)
    smem = pl.BlockSpec(memory_space=pltpu.SMEM)
    out = jax.ShapeDtypeStruct((y_n, z_n, x_n, part_l, width), BF)

    def add(parts):
        total = parts[0].astype(F32)
        for p in parts[1:]:
            total = total + p.astype(F32)
        return total

    chips = []
    for var in range(n_var):
        index, place = where_var[var]
        if index and place == 0:
            early = jnp.stack(chips, axis=3)
            early = add([early[0]] + [shift_y(early[s], s) for s in range(1, y_n)]).astype(BF)
            chips = []
        near, far = pl.pallas_call(
            functools.partial(member_kernel, var=var, slot_of_var=place),
            out_shape=(out, out),
            in_specs=[smem, smem, vmem, vmem, vmem, vmem, vmem, vmem,
                      pl.BlockSpec(memory_space=pl.ANY)],
            out_specs=(vmem, vmem),
            scratch_shapes=[
                pltpu.VMEM(turned_tiles.shape, BF),
                pltpu.VMEM((columns, width, members * levels), BF),
                pltpu.VMEM((columns, members * width, levels), BF),
                pltpu.SemaphoreType.DMA((4,)),
            ],
            compiler_params=pltpu.CompilerParams(vmem_limit_bytes=40 << 20),
        )(where, tile_col, arrived[index], mine, other, vert_t, vert_root, mask, turned_tiles)
        chips.append(add([near, swap(far)]).astype(BF))
    late = jnp.stack(chips, axis=3)
    late = add([late[0]] + [shift_y(late[s], s) for s in range(1, y_n)]).astype(BF)
    held = jnp.concatenate([early, late], axis=2)
    held = add([held[0]] + [shift_z(held[s], s) for s in range(1, z_n)]).astype(BF)
    held = add([held[0]] + [shift_x(held[s], s) for s in range(1, x_n)])
    return (held / (members_all - 1)).astype(BF)


def solution(mesh):
    y_n = mesh.shape["mem"]
    side = int(round((mesh.shape["col"] // CORES) ** 0.5))
    placed = (P("mem", None, None, "col"), P(None, "mem", "col"), P(), P(), P(), P())
    return jax.shard_map(
        functools.partial(on_device, y_n=y_n, z_n=side, x_n=side),
        mesh=mesh, in_specs=placed, out_specs=P(None, "mem", "col"), check_vma=False,
    )
```

```python
import functools

import jax
import jax.numpy as jnp
from jax import lax
from jax.experimental import pallas as pl
from jax.experimental.pallas import tpu as pltpu
from jax.sharding import PartitionSpec as P


BF = jnp.bfloat16
F32 = jnp.float32
CORES = 2
FLOOR = 2
UNROLL = 8
LIFT_UNROLL = 4


def member_kernel(
    where_ref, cols_ref, ens_ref, mine_ref, other_ref, vt_ref, vn_ref, mask_ref, tiles_ref,
    near_ref, far_ref, ens_buf, tile_buf, lifted, spread_buf, ens_sems, tile_sems, *, var, slot_of_var,
):
    n_blocks, members, levels, width = ens_buf.shape
    y_n, z_n, x_n = mine_ref.shape[0], mine_ref.shape[1], mine_ref.shape[2]
    part_l = mine_ref.shape[4]
    slots = cols_ref.shape[1]
    my_y, my_z, my_x, my_c = where_ref[0], where_ref[1], where_ref[2], where_ref[3]
    n_copies = z_n
    per_copy = n_blocks // n_copies

    def ens_copy(off_z):
        span = pl.ds(lax.rem(my_z + off_z, z_n) * per_copy, per_copy)
        return pltpu.make_async_copy(
            ens_ref.at[span, :, slot_of_var], ens_buf.at[span], ens_sems.at[off_z]
        )

    def tile_copy(piece):
        span = pl.ds(piece * per_copy, per_copy)
        return pltpu.make_async_copy(tiles_ref.at[span], tile_buf.at[span], tile_sems.at[piece])

    for piece in range(n_copies):
        ens_copy(piece).start()
    for piece in range(n_copies):
        tile_copy(piece).start()

    def seat_of(step):
        off_z, off_x = step // x_n, step % x_n
        z = lax.rem(my_z + off_z, z_n)
        x = lax.rem(my_x + off_x, x_n)
        return off_z, off_x, (z * x_n + x) * CORES

    def lift_block(source_ref, block, in_z, in_x):
        halves = []
        for m in range(members):
            bands = []
            for quarter in range(y_n):
                off_y = lax.rem(my_y - quarter + y_n, y_n)
                incr = source_ref[off_y, in_z, in_x, var].astype(F32)
                rows = ens_buf[block, m, quarter * part_l:(quarter + 1) * part_l, :]
                bands.append((rows.astype(F32) * incr).astype(BF))
            halves.append(jnp.concatenate(bands, axis=0))
        weighted = jnp.concatenate(halves, axis=1)
        lift = jnp.dot(vt_ref[var], weighted, preferred_element_type=F32).astype(BF)
        for m in range(members):
            lifted[block, :, m * levels:(m + 1) * levels] = jnp.swapaxes(
                lift[:, m * width:(m + 1) * width], 0, 1
            )

    def lift_step(step, carry):
        off_z, off_x, base = seat_of(step)
        in_z = lax.rem(z_n - off_z, z_n)
        in_x = lax.rem(x_n - off_x, x_n)
        lift_block(mine_ref, base + my_c, in_z, in_x)
        lift_block(other_ref, base + 1 - my_c, in_z, in_x)
        return carry

    for off_z in range(z_n):
        ens_copy(off_z).wait()
        lax.fori_loop(off_z * x_n, (off_z + 1) * x_n, lift_step, 0, unroll=LIFT_UNROLL)

    def spread_block(block):
        parts = []
        for slot in range(slots):
            picked = lifted[cols_ref[block, slot]]
            if slot >= FLOOR:
                picked = picked * mask_ref[slot - FLOOR]
            parts.append(picked)
        spread = jnp.dot(
            tile_buf[block], jnp.concatenate(parts, axis=0), preferred_element_type=F32
        ).astype(BF)
        for m in range(members):
            spread_buf[block, m * width:(m + 1) * width, :] = spread[:, m * levels:(m + 1) * levels]

    def spread_step(step, carry):
        spread_block(step)
        return carry

    for piece in range(n_copies):
        tile_copy(piece).wait()
        lax.fori_loop(piece * per_copy, (piece + 1) * per_copy, spread_step, 0, unroll=UNROLL)

    def lower_block(target_ref, block, off_z, off_x):
        beside = spread_buf[block]
        lowered = lax.dot_general(
            vn_ref[var], beside, (((1,), (1,)), ((), ())), preferred_element_type=F32
        )
        total = None
        for m in range(members):
            term = ens_buf[block, m].astype(F32) * lowered[:, m * width:(m + 1) * width]
            total = term if total is None else total + term
        total = total.astype(BF)
        for quarter in range(y_n):
            off_y = lax.rem(quarter - my_y + y_n, y_n)
            target_ref[off_y, off_z, off_x] = total[quarter * part_l:(quarter + 1) * part_l, :]

    def lower_step(step, carry):
        off_z, off_x, base = seat_of(step)
        lower_block(near_ref, base + my_c, off_z, off_x)
        lower_block(far_ref, base + 1 - my_c, off_z, off_x)
        return carry

    lax.fori_loop(0, n_blocks // CORES, lower_step, 0, unroll=8)


def on_device(
    ensemble, increment, vert_root, tiles, tile_col, level_reach, *, y_n, z_n, x_n
):
    columns = lax.axis_size("col")
    members_all = ensemble.shape[0] * lax.axis_size("mem")
    members = ensemble.shape[0] // columns
    n_var, levels, width = ensemble.shape[1:]
    part_l = increment.shape[1]
    slots = tiles.shape[1]
    col = lax.axis_index("col")
    my_y = lax.axis_index("mem")
    my_z, my_x, my_c = col // (x_n * CORES), (col // CORES) % x_n, col % CORES
    where = jnp.stack([my_y, my_z, my_x, my_c]).astype(jnp.int32)

    def seat(z, x, c):
        return ((z % z_n) * x_n + x % x_n) * CORES + c

    seats = [(z, x, c) for z in range(z_n) for x in range(x_n) for c in range(CORES)]

    def shift_y(a, s):
        return lax.ppermute(a, "mem", [(i, (i + s) % y_n) for i in range(y_n)])

    def shift_z(a, s):
        return lax.ppermute(a, "col", [(seat(*p), seat(p[0] + s, p[1], p[2])) for p in seats])

    def shift_x(a, s):
        return lax.ppermute(a, "col", [(seat(*p), seat(p[0], p[1] + s, p[2])) for p in seats])

    def swap(a):
        return lax.ppermute(a, "col", [(seat(*p), seat(p[0], p[1], 1 - p[2])) for p in seats])

    def collect(a, shift, n):
        return jnp.stack([a] + [shift(a, s) for s in range(1, n)])

    by_member = ensemble.reshape(columns, members, n_var, levels, width)
    groups = ((0, 1), (2,))
    pieces = [by_member[:, :, group[0]:group[-1] + 1] for group in groups]
    where_var = {
        var: (index, place) for index, group in enumerate(groups) for place, var in enumerate(group)
    }

    mine = collect(increment, shift_x, x_n)
    pieces[0], mine = lax.optimization_barrier((pieces[0], mine))
    mine = collect(mine, shift_z, z_n)
    arrived = [lax.all_to_all(pieces[0], "col", 0, 0)]
    mine, pieces[1], tiles = lax.optimization_barrier((mine, pieces[1], tiles))
    turned_tiles = jnp.transpose(tiles, (0, 3, 1, 2)).reshape(columns, width, slots * width)
    mine = collect(mine, shift_y, y_n)
    mine, turned_tiles = lax.optimization_barrier((mine, turned_tiles))
    other = swap(mine)
    pieces[1], arrived[0] = lax.optimization_barrier((pieces[1], arrived[0]))
    arrived.append(lax.all_to_all(pieces[1], "col", 0, 0))

    vert_t = jnp.swapaxes(vert_root, 1, 2)
    active = (
        jnp.arange(FLOOR, slots, dtype=jnp.int32)[:, None] < level_reach[None, :]
    ).astype(BF)
    mask = jnp.tile(active, (1, members))[:, None, :]

    vmem = pl.BlockSpec(memory_space=pltpu.VMEM)
    smem = pl.BlockSpec(memory_space=pltpu.SMEM)
    anywhere = pl.BlockSpec(memory_space=pl.ANY)
    out = jax.ShapeDtypeStruct((y_n, z_n, x_n, part_l, width), BF)

    def add(parts):
        total = parts[0].astype(F32)
        for p in parts[1:]:
            total = total + p.astype(F32)
        return total

    chips = []
    for var in range(n_var):
        index, place = where_var[var]
        if index and place == 0:
            early = jnp.stack(chips, axis=3)
            early = add([early[0]] + [shift_y(early[s], s) for s in range(1, y_n)]).astype(BF)
            chips = []
        near, far = pl.pallas_call(
            functools.partial(member_kernel, var=var, slot_of_var=place),
            out_shape=(out, out),
            in_specs=[smem, smem, anywhere, vmem, vmem, vmem, vmem, vmem,
                      anywhere],
            out_specs=(vmem, vmem),
            scratch_shapes=[
                pltpu.VMEM((columns, members, levels, width), BF),
                pltpu.VMEM(turned_tiles.shape, BF),
                pltpu.VMEM((columns, width, members * levels), BF),
                pltpu.VMEM((columns, members * width, levels), BF),
                pltpu.SemaphoreType.DMA((z_n,)),
                pltpu.SemaphoreType.DMA((z_n,)),
            ],
            compiler_params=pltpu.CompilerParams(vmem_limit_bytes=40 << 20),
        )(where, tile_col, arrived[index], mine, other, vert_t, vert_root, mask, turned_tiles)
        chips.append(add([near, swap(far)]).astype(BF))
    late = jnp.stack(chips, axis=3)
    late = add([late[0]] + [shift_y(late[s], s) for s in range(1, y_n)]).astype(BF)
    held = jnp.concatenate([early, late], axis=2)
    held = add([held[0]] + [shift_z(held[s], s) for s in range(1, z_n)]).astype(BF)
    held = add([held[0]] + [shift_x(held[s], s) for s in range(1, x_n)])
    return (held / (members_all - 1)).astype(BF)


def solution(mesh):
    y_n = mesh.shape["mem"]
    side = int(round((mesh.shape["col"] // CORES) ** 0.5))
    placed = (P("mem", None, None, "col"), P(None, "mem", "col"), P(), P(), P(), P())
    return jax.shard_map(
        functools.partial(on_device, y_n=y_n, z_n=side, x_n=side),
        mesh=mesh, in_specs=placed, out_specs=P(None, "mem", "col"), check_vma=False,
    )
```

```python
import functools

import jax
import jax.numpy as jnp
from jax import lax
from jax.experimental import pallas as pl
from jax.experimental.pallas import tpu as pltpu
from jax.sharding import PartitionSpec as P


BF = jnp.bfloat16
F32 = jnp.float32
CORES = 2
FLOOR = 2
UNROLL = 8
LIFT_UNROLL = 4


def member_kernel(
    where_ref, cols_ref, ens_ref, mine_ref, other_ref, vt_ref, vn_ref, mask_ref, tiles_ref,
    near_ref, far_ref, ens_buf, tile_buf, lifted, spread_buf, ens_sems, tile_sems, *, var, slot_of_var,
):
    n_blocks, members, levels, width = ens_buf.shape
    y_n, z_n, x_n = mine_ref.shape[0], mine_ref.shape[1], mine_ref.shape[2]
    part_l = mine_ref.shape[4]
    slots = cols_ref.shape[1]
    my_y, my_z, my_x, my_c = where_ref[0], where_ref[1], where_ref[2], where_ref[3]
    n_copies = z_n
    per_copy = n_blocks // n_copies

    def ens_copy(off_z):
        span = pl.ds(lax.bitwise_xor(my_z, off_z) * per_copy, per_copy)
        return pltpu.make_async_copy(
            ens_ref.at[span, :, slot_of_var], ens_buf.at[span], ens_sems.at[off_z]
        )

    def tile_copy(piece):
        span = pl.ds(piece * per_copy, per_copy)
        return pltpu.make_async_copy(tiles_ref.at[span], tile_buf.at[span], tile_sems.at[piece])

    for piece in range(n_copies):
        ens_copy(piece).start()
    for piece in range(n_copies):
        tile_copy(piece).start()

    def seat_of(step):
        off_z, off_x = step // x_n, step % x_n
        z = lax.bitwise_xor(my_z, off_z)
        x = lax.bitwise_xor(my_x, off_x)
        return off_z, off_x, (z * x_n + x) * CORES

    def lift_block(source_ref, block, off_z, off_x):
        halves = []
        for m in range(members):
            bands = []
            for quarter in range(y_n):
                off_y = lax.bitwise_xor(my_y, quarter)
                incr = source_ref[off_y, off_z, off_x, var].astype(F32)
                rows = ens_buf[block, m, quarter * part_l:(quarter + 1) * part_l, :]
                bands.append((rows.astype(F32) * incr).astype(BF))
            halves.append(jnp.concatenate(bands, axis=0))
        weighted = jnp.concatenate(halves, axis=1)
        lift = jnp.dot(vt_ref[var], weighted, preferred_element_type=F32).astype(BF)
        for m in range(members):
            lifted[block, :, m * levels:(m + 1) * levels] = jnp.swapaxes(
                lift[:, m * width:(m + 1) * width], 0, 1
            )

    def lift_step(step, carry):
        off_z, off_x, base = seat_of(step)
        lift_block(mine_ref, base + my_c, off_z, off_x)
        lift_block(other_ref, base + 1 - my_c, off_z, off_x)
        return carry

    for off_z in range(z_n):
        ens_copy(off_z).wait()
        lax.fori_loop(off_z * x_n, (off_z + 1) * x_n, lift_step, 0, unroll=LIFT_UNROLL)

    def spread_block(block):
        parts = []
        for slot in range(slots):
            picked = lifted[cols_ref[block, slot]]
            if slot >= FLOOR:
                picked = picked * mask_ref[slot - FLOOR]
            parts.append(picked)
        spread = jnp.dot(
            tile_buf[block], jnp.concatenate(parts, axis=0), preferred_element_type=F32
        ).astype(BF)
        for m in range(members):
            spread_buf[block, m * width:(m + 1) * width, :] = spread[:, m * levels:(m + 1) * levels]

    def spread_step(step, carry):
        spread_block(step)
        return carry

    for piece in range(n_copies):
        tile_copy(piece).wait()
        lax.fori_loop(piece * per_copy, (piece + 1) * per_copy, spread_step, 0, unroll=UNROLL)

    def lower_block(target_ref, block, off_z, off_x):
        beside = spread_buf[block]
        lowered = lax.dot_general(
            vn_ref[var], beside, (((1,), (1,)), ((), ())), preferred_element_type=F32
        )
        total = None
        for m in range(members):
            term = ens_buf[block, m].astype(F32) * lowered[:, m * width:(m + 1) * width]
            total = term if total is None else total + term
        total = total.astype(BF)
        for quarter in range(y_n):
            off_y = lax.bitwise_xor(my_y, quarter)
            target_ref[off_y, off_z, off_x] = total[quarter * part_l:(quarter + 1) * part_l, :]

    def lower_step(step, carry):
        off_z, off_x, base = seat_of(step)
        lower_block(near_ref, base + my_c, off_z, off_x)
        lower_block(far_ref, base + 1 - my_c, off_z, off_x)
        return carry

    lax.fori_loop(0, n_blocks // CORES, lower_step, 0, unroll=8)


def cut_kernel(source_ref, piece_ref, stage, in_sems, out_sems, *, low):
    parts = in_sems.shape[0]
    blocks, _, count = piece_ref.shape[:3]
    per = blocks // parts

    def fetch(i):
        span = pl.ds(i * per, per)
        return pltpu.make_async_copy(
            source_ref.at[span, :, pl.ds(low, count)], stage.at[span], in_sems.at[i]
        )

    def put(i):
        span = pl.ds(i * per, per)
        return pltpu.make_async_copy(stage.at[span], piece_ref.at[span], out_sems.at[i])

    for i in range(parts):
        fetch(i).start()
    for i in range(parts):
        fetch(i).wait()
        put(i).start()
    for i in range(parts):
        put(i).wait()


def on_device(
    ensemble, increment, vert_root, tiles, tile_col, level_reach, *, y_n, z_n, x_n
):
    columns = lax.axis_size("col")
    members_all = ensemble.shape[0] * lax.axis_size("mem")
    members = ensemble.shape[0] // columns
    n_var, levels, width = ensemble.shape[1:]
    part_l = increment.shape[1]
    slots = tiles.shape[1]
    col = lax.axis_index("col")
    my_y = lax.axis_index("mem")
    my_z, my_x, my_c = col // (x_n * CORES), (col // CORES) % x_n, col % CORES
    where = jnp.stack([my_y, my_z, my_x, my_c]).astype(jnp.int32)

    def seat(z, x, c):
        return (z * x_n + x) * CORES + c

    seats = [(z, x, c) for z in range(z_n) for x in range(x_n) for c in range(CORES)]

    def shift_y(a, s):
        return lax.ppermute(a, "mem", [(i, i ^ s) for i in range(y_n)])

    def shift_z(a, s):
        return lax.ppermute(a, "col", [(seat(*p), seat(p[0] ^ s, p[1], p[2])) for p in seats])

    def shift_x(a, s):
        return lax.ppermute(a, "col", [(seat(*p), seat(p[0], p[1] ^ s, p[2])) for p in seats])

    def swap(a):
        return lax.ppermute(a, "col", [(seat(*p), seat(p[0], p[1], 1 - p[2])) for p in seats])

    def collect(a, shift, n):
        return jnp.stack([a] + [shift(a, s) for s in range(1, n)])

    by_member = ensemble.reshape(columns, members, n_var, levels, width)
    groups = ((0, 1), (2,))
    pieces = [by_member[:, :, group[0]:group[-1] + 1] for group in groups]
    pieces[0] = pl.pallas_call(
        functools.partial(cut_kernel, low=groups[0][0]),
        out_shape=jax.ShapeDtypeStruct(pieces[0].shape, BF),
        in_specs=[pl.BlockSpec(memory_space=pl.ANY)],
        out_specs=pl.BlockSpec(memory_space=pl.ANY),
        scratch_shapes=[
            pltpu.VMEM(pieces[0].shape, BF),
            pltpu.SemaphoreType.DMA((8,)),
            pltpu.SemaphoreType.DMA((8,)),
        ],
        compiler_params=pltpu.CompilerParams(vmem_limit_bytes=60 << 20),
        name="cut",
    )(by_member)
    where_var = {
        var: (index, place) for index, group in enumerate(groups) for place, var in enumerate(group)
    }

    mine = collect(increment, shift_x, x_n)
    pieces[0], mine = lax.optimization_barrier((pieces[0], mine))
    mine = collect(mine, shift_z, z_n)
    arrived = [lax.all_to_all(pieces[0], "col", 0, 0)]
    mine, pieces[1], tiles = lax.optimization_barrier((mine, pieces[1], tiles))
    turned_tiles = jnp.transpose(tiles, (0, 3, 1, 2)).reshape(columns, width, slots * width)
    mine = collect(mine, shift_y, y_n)
    mine, turned_tiles = lax.optimization_barrier((mine, turned_tiles))
    other = swap(mine)
    pieces[1], arrived[0] = lax.optimization_barrier((pieces[1], arrived[0]))
    arrived.append(lax.all_to_all(pieces[1], "col", 0, 0))

    vert_t = jnp.swapaxes(vert_root, 1, 2)
    active = (
        jnp.arange(FLOOR, slots, dtype=jnp.int32)[:, None] < level_reach[None, :]
    ).astype(BF)
    mask = jnp.tile(active, (1, members))[:, None, :]

    vmem = pl.BlockSpec(memory_space=pltpu.VMEM)
    smem = pl.BlockSpec(memory_space=pltpu.SMEM)
    anywhere = pl.BlockSpec(memory_space=pl.ANY)
    out = jax.ShapeDtypeStruct((y_n, z_n, x_n, part_l, width), BF)

    def add(parts):
        total = parts[0].astype(F32)
        for p in parts[1:]:
            total = total + p.astype(F32)
        return total

    chips = []
    for var in range(n_var):
        index, place = where_var[var]
        if index and place == 0:
            early = jnp.stack(chips, axis=3)
            early = add([early[0]] + [shift_y(early[s], s) for s in range(1, y_n)]).astype(BF)
            chips = []
        near, far = pl.pallas_call(
            functools.partial(member_kernel, var=var, slot_of_var=place),
            out_shape=(out, out),
            in_specs=[smem, smem, anywhere, vmem, vmem, vmem, vmem, vmem,
                      anywhere],
            out_specs=(vmem, vmem),
            scratch_shapes=[
                pltpu.VMEM((columns, members, levels, width), BF),
                pltpu.VMEM(turned_tiles.shape, BF),
                pltpu.VMEM((columns, width, members * levels), BF),
                pltpu.VMEM((columns, members * width, levels), BF),
                pltpu.SemaphoreType.DMA((z_n,)),
                pltpu.SemaphoreType.DMA((z_n,)),
            ],
            compiler_params=pltpu.CompilerParams(vmem_limit_bytes=40 << 20),
        )(where, tile_col, arrived[index], mine, other, vert_t, vert_root, mask, turned_tiles)
        chips.append(add([near, swap(far)]).astype(BF))
    late = jnp.stack(chips, axis=3)
    late = add([late[0]] + [shift_y(late[s], s) for s in range(1, y_n)]).astype(BF)
    held = jnp.concatenate([early, late], axis=2)
    held = add([held[0]] + [shift_z(held[s], s) for s in range(1, z_n)]).astype(BF)
    held = add([held[0]] + [shift_x(held[s], s) for s in range(1, x_n)])
    return (held / (members_all - 1)).astype(BF)


def solution(mesh):
    y_n = mesh.shape["mem"]
    side = int(round((mesh.shape["col"] // CORES) ** 0.5))
    placed = (P("mem", None, None, "col"), P(None, "mem", "col"), P(), P(), P(), P())
    return jax.shard_map(
        functools.partial(on_device, y_n=y_n, z_n=side, x_n=side),
        mesh=mesh, in_specs=placed, out_specs=P(None, "mem", "col"), check_vma=False,
    )
```

```python
import functools

import jax
import jax.numpy as jnp
from jax import lax
from jax.experimental import pallas as pl
from jax.experimental.pallas import tpu as pltpu
from jax.sharding import PartitionSpec as P


BF = jnp.bfloat16
F32 = jnp.float32
CORES = 2
FLOOR = 2
UNROLL = 8
LIFT_UNROLL = 4


def member_kernel(
    where_ref, cols_ref, ens_ref, mine_ref, other_ref, vt_ref, vn_ref, mask_ref, tiles_ref,
    near_ref, far_ref, ens_buf, tile_buf, lifted, spread_buf, ens_sems, tile_sems, *, var, slot_of_var,
):
    n_blocks, members, levels, width = ens_buf.shape
    y_n, z_n, x_n = mine_ref.shape[0], mine_ref.shape[1], mine_ref.shape[2]
    part_l = mine_ref.shape[4]
    slots = cols_ref.shape[1]
    my_y, my_z, my_x, my_c = where_ref[0], where_ref[1], where_ref[2], where_ref[3]
    n_copies = z_n
    per_copy = n_blocks // n_copies

    def ens_copy(off_z):
        span = pl.ds(lax.bitwise_xor(my_z, off_z) * per_copy, per_copy)
        return pltpu.make_async_copy(
            ens_ref.at[span, :, slot_of_var], ens_buf.at[span], ens_sems.at[off_z]
        )

    def tile_copy(piece):
        span = pl.ds(piece * per_copy, per_copy)
        return pltpu.make_async_copy(tiles_ref.at[span], tile_buf.at[span], tile_sems.at[piece])

    for piece in range(n_copies):
        ens_copy(piece).start()
    for piece in range(n_copies):
        tile_copy(piece).start()

    def seat_of(step):
        off_z, off_x = step // x_n, step % x_n
        z = lax.bitwise_xor(my_z, off_z)
        x = lax.bitwise_xor(my_x, off_x)
        return off_z, off_x, (z * x_n + x) * CORES

    def lift_block(source_ref, block, off_z, off_x):
        halves = []
        for m in range(members):
            bands = []
            for quarter in range(y_n):
                off_y = lax.bitwise_xor(my_y, quarter)
                incr = source_ref[off_y, off_z, off_x, var].astype(F32)
                rows = ens_buf[block, m, quarter * part_l:(quarter + 1) * part_l, :]
                bands.append((rows.astype(F32) * incr).astype(BF))
            halves.append(jnp.concatenate(bands, axis=0))
        weighted = jnp.concatenate(halves, axis=1)
        lift = jnp.dot(vt_ref[var], weighted, preferred_element_type=F32).astype(BF)
        for m in range(members):
            lifted[block, :, m * levels:(m + 1) * levels] = jnp.swapaxes(
                lift[:, m * width:(m + 1) * width], 0, 1
            )

    def lift_step(step, carry):
        off_z, off_x, base = seat_of(step)
        lift_block(mine_ref, base + my_c, off_z, off_x)
        lift_block(other_ref, base + 1 - my_c, off_z, off_x)
        return carry

    for off_z in range(z_n):
        ens_copy(off_z).wait()
        lax.fori_loop(off_z * x_n, (off_z + 1) * x_n, lift_step, 0, unroll=LIFT_UNROLL)

    def spread_block(block):
        parts = []
        for slot in range(slots):
            picked = lifted[cols_ref[block, slot]]
            if slot >= FLOOR:
                picked = picked * mask_ref[slot - FLOOR]
            parts.append(picked)
        spread = jnp.dot(
            tile_buf[block], jnp.concatenate(parts, axis=0), preferred_element_type=F32
        ).astype(BF)
        for m in range(members):
            spread_buf[block, m * width:(m + 1) * width, :] = spread[:, m * levels:(m + 1) * levels]

    def spread_step(step, carry):
        spread_block(step)
        return carry

    for piece in range(n_copies):
        tile_copy(piece).wait()
        lax.fori_loop(piece * per_copy, (piece + 1) * per_copy, spread_step, 0, unroll=UNROLL)

    def lower_block(target_ref, block, off_z, off_x):
        beside = spread_buf[block]
        lowered = lax.dot_general(
            vn_ref[var], beside, (((1,), (1,)), ((), ())), preferred_element_type=F32
        )
        total = None
        for m in range(members):
            term = ens_buf[block, m].astype(F32) * lowered[:, m * width:(m + 1) * width]
            total = term if total is None else total + term
        total = total.astype(BF)
        for quarter in range(y_n):
            off_y = lax.bitwise_xor(my_y, quarter)
            target_ref[off_y, off_z, off_x] = total[quarter * part_l:(quarter + 1) * part_l, :]

    def lower_step(step, carry):
        off_z, off_x, base = seat_of(step)
        lower_block(near_ref, base + my_c, off_z, off_x)
        lower_block(far_ref, base + 1 - my_c, off_z, off_x)
        return carry

    lax.fori_loop(0, n_blocks // CORES, lower_step, 0, unroll=8)


def far_first(n):
    return sorted(range(1, n), key=lambda s: (s != n // 2, -s))


def cut_kernel(source_ref, piece_ref, stage, in_sems, out_sems, *, low):
    parts = in_sems.shape[0]
    blocks, _, count = piece_ref.shape[:3]
    per = blocks // parts

    def fetch(i):
        span = pl.ds(i * per, per)
        return pltpu.make_async_copy(
            source_ref.at[span, :, pl.ds(low, count)], stage.at[span], in_sems.at[i]
        )

    def put(i):
        span = pl.ds(i * per, per)
        return pltpu.make_async_copy(stage.at[span], piece_ref.at[span], out_sems.at[i])

    for i in range(parts):
        fetch(i).start()
    for i in range(parts):
        fetch(i).wait()
        put(i).start()
    for i in range(parts):
        put(i).wait()


def on_device(
    ensemble, increment, vert_root, tiles, tile_col, level_reach, *, y_n, z_n, x_n
):
    columns = lax.axis_size("col")
    members_all = ensemble.shape[0] * lax.axis_size("mem")
    members = ensemble.shape[0] // columns
    n_var, levels, width = ensemble.shape[1:]
    part_l = increment.shape[1]
    slots = tiles.shape[1]
    col = lax.axis_index("col")
    my_y = lax.axis_index("mem")
    my_z, my_x, my_c = col // (x_n * CORES), (col // CORES) % x_n, col % CORES
    where = jnp.stack([my_y, my_z, my_x, my_c]).astype(jnp.int32)

    def seat(z, x, c):
        return (z * x_n + x) * CORES + c

    seats = [(z, x, c) for z in range(z_n) for x in range(x_n) for c in range(CORES)]

    def shift_y(a, s):
        return lax.ppermute(a, "mem", [(i, i ^ s) for i in range(y_n)])

    def shift_z(a, s):
        return lax.ppermute(a, "col", [(seat(*p), seat(p[0] ^ s, p[1], p[2])) for p in seats])

    def shift_x(a, s):
        return lax.ppermute(a, "col", [(seat(*p), seat(p[0], p[1] ^ s, p[2])) for p in seats])

    def swap(a):
        return lax.ppermute(a, "col", [(seat(*p), seat(p[0], p[1], 1 - p[2])) for p in seats])

    def collect(a, shift, n):
        got = {s: shift(a, s) for s in far_first(n)}
        return jnp.stack([a] + [got[s] for s in range(1, n)])

    by_member = ensemble.reshape(columns, members, n_var, levels, width)
    groups = ((0, 1), (2,))
    pieces = [by_member[:, :, group[0]:group[-1] + 1] for group in groups]
    pieces[0] = pl.pallas_call(
        functools.partial(cut_kernel, low=groups[0][0]),
        out_shape=jax.ShapeDtypeStruct(pieces[0].shape, BF),
        in_specs=[pl.BlockSpec(memory_space=pl.ANY)],
        out_specs=pl.BlockSpec(memory_space=pl.ANY),
        scratch_shapes=[
            pltpu.VMEM(pieces[0].shape, BF),
            pltpu.SemaphoreType.DMA((8,)),
            pltpu.SemaphoreType.DMA((8,)),
        ],
        compiler_params=pltpu.CompilerParams(vmem_limit_bytes=60 << 20),
        name="cut",
    )(by_member)
    where_var = {
        var: (index, place) for index, group in enumerate(groups) for place, var in enumerate(group)
    }

    mine = collect(increment, shift_x, x_n)
    pieces[0], mine = lax.optimization_barrier((pieces[0], mine))
    mine = collect(mine, shift_z, z_n)
    arrived = [lax.all_to_all(pieces[0], "col", 0, 0)]
    mine, pieces[1], tiles = lax.optimization_barrier((mine, pieces[1], tiles))
    turned_tiles = jnp.transpose(tiles, (0, 3, 1, 2)).reshape(columns, width, slots * width)
    mine = collect(mine, shift_y, y_n)
    mine, turned_tiles = lax.optimization_barrier((mine, turned_tiles))
    other = swap(mine)
    pieces[1], arrived[0] = lax.optimization_barrier((pieces[1], arrived[0]))
    arrived.append(lax.all_to_all(pieces[1], "col", 0, 0))

    vert_t = jnp.swapaxes(vert_root, 1, 2)
    active = (
        jnp.arange(FLOOR, slots, dtype=jnp.int32)[:, None] < level_reach[None, :]
    ).astype(BF)
    mask = jnp.tile(active, (1, members))[:, None, :]

    vmem = pl.BlockSpec(memory_space=pltpu.VMEM)
    smem = pl.BlockSpec(memory_space=pltpu.SMEM)
    anywhere = pl.BlockSpec(memory_space=pl.ANY)
    out = jax.ShapeDtypeStruct((y_n, z_n, x_n, part_l, width), BF)

    def add(parts):
        total = parts[0].astype(F32)
        for p in parts[1:]:
            total = total + p.astype(F32)
        return total

    chips = []
    for var in range(n_var):
        index, place = where_var[var]
        if index and place == 0:
            early = jnp.stack(chips, axis=3)
            early = add([early[0]] + [shift_y(early[s], s) for s in far_first(y_n)]).astype(BF)
            chips = []
        near, far = pl.pallas_call(
            functools.partial(member_kernel, var=var, slot_of_var=place),
            out_shape=(out, out),
            in_specs=[smem, smem, anywhere, vmem, vmem, vmem, vmem, vmem,
                      anywhere],
            out_specs=(vmem, vmem),
            scratch_shapes=[
                pltpu.VMEM((columns, members, levels, width), BF),
                pltpu.VMEM(turned_tiles.shape, BF),
                pltpu.VMEM((columns, width, members * levels), BF),
                pltpu.VMEM((columns, members * width, levels), BF),
                pltpu.SemaphoreType.DMA((z_n,)),
                pltpu.SemaphoreType.DMA((z_n,)),
            ],
            compiler_params=pltpu.CompilerParams(vmem_limit_bytes=40 << 20),
        )(where, tile_col, arrived[index], mine, other, vert_t, vert_root, mask, turned_tiles)
        chips.append(add([near, swap(far)]).astype(BF))
    late = jnp.stack(chips, axis=3)
    late = add([late[0]] + [shift_y(late[s], s) for s in far_first(y_n)]).astype(BF)
    held = jnp.concatenate([early, late], axis=2)
    held = add([held[0]] + [shift_z(held[s], s) for s in far_first(z_n)]).astype(BF)
    held = add([held[0]] + [shift_x(held[s], s) for s in far_first(x_n)])
    return (held / (members_all - 1)).astype(BF)


def solution(mesh):
    y_n = mesh.shape["mem"]
    side = int(round((mesh.shape["col"] // CORES) ** 0.5))
    placed = (P("mem", None, None, "col"), P(None, "mem", "col"), P(), P(), P(), P())
    return jax.shard_map(
        functools.partial(on_device, y_n=y_n, z_n=side, x_n=side),
        mesh=mesh, in_specs=placed, out_specs=P(None, "mem", "col"), check_vma=False,
    )
```
